32 devices in a mesh: rep: 4 (over z), dp: 2 (over y), cp: 4 (over x, core).
Axes of the slice: x: 2, y: 2, z: 4, core: 2. Of those that a mesh axis runs over, the one named last changes fastest.
Arguments:
- block_in: bfloat16 [8, 1024, 2048], P(('rep', 'dp'), 'cp'), may hold values from -6 to 6
- positions: int32 [8, 1024], P(('rep', 'dp')), may hold values from 0 to 1023, as said below
- norm_attn: bfloat16 [2048], P(('dp', 'cp')), may hold values from 0.5 to 1.5
- w_query: bfloat16 [2048, 2048], P(('dp', 'cp')), may hold values from -0.125 to 0.125
- key_weight: bfloat16 [2048, 512], P(('dp', 'cp')), may hold values from -0.125 to 0.125
- w_value: bfloat16 [2048, 512], P(('dp', 'cp')), may hold values from -0.125 to 0.125
- w_out: bfloat16 [2048, 2048], P(('dp', 'cp')), may hold values from -2 to 2
- norm_ffn: bfloat16 [2048], P(('dp', 'cp')), may hold values from 0.5 to 1.5
- w_gate: bfloat16 [2048, 8192], P(('dp', 'cp')), may hold values from -0.125 to 0.125
- w_up: bfloat16 [2048, 8192], P(('dp', 'cp')), may hold values from -0.125 to 0.125
- w_down: bfloat16 [8192, 2048], P(('dp', 'cp')), may hold values from -0.0625 to 0.0625
- cotangent: bfloat16 [8, 1024, 2048], P(('rep', 'dp'), 'cp'), may hold values from -6 to 6
Outputs:
- block_out: bfloat16 [8, 1024, 2048], P(('rep', 'dp'), 'cp')
- input_grad: bfloat16 [8, 1024, 2048], P(('rep', 'dp'), 'cp')
- norm_attn_grad: float32 [2048], P(('dp', 'cp'))
- w_query_grad: float32 [2048, 2048], P(('dp', 'cp'))
- w_key_grad: float32 [2048, 512], P(('dp', 'cp'))
- w_value_grad: float32 [2048, 512], P(('dp', 'cp'))
- w_out_grad: float32 [2048, 2048], P(('dp', 'cp'))
- norm_ffn_grad: float32 [2048], P(('dp', 'cp'))
- w_gate_grad: float32 [2048, 8192], P(('dp', 'cp'))
- w_up_grad: float32 [2048, 8192], P(('dp', 'cp'))
- w_down_grad: float32 [8192, 2048], P(('dp', 'cp'))
The draws below stay inside these ranges and needn't reach their ends.
Inputs may be any that keep to these rules, and one draw needn't show every extreme that they name: Each row of positions is a permutation of 0 to 1023 made of runs of 64 consecutive positions that start at multiples of 64.
All inputs are finite; a program needn't handle non-finite values.
Results may differ from the reference program's by a relative error of at most 0.02.
Values may be sent and summed in bfloat16 or wider, within the bound.
A program may use at most 512 MiB of HBM per device.

```python
import jax
import jax.numpy as jnp
from jax import lax

D = 2048
QUERY_HEADS = 32
KEY_VALUE_HEADS = 8
HEAD_SIZE = 64
FF = 8192
BLK = 64
QW = 2048
KEY_FEATURES = 512
LEN = 1024
SEQS = 8


def draw_positions(key, part):
    seq_keys = jax.random.split(jax.random.fold_in(key, 11), SEQS)
    orders = jax.vmap(lambda seq_key: jax.random.permutation(seq_key, LEN // BLK))(seq_keys)
    offsets = jnp.arange(BLK, dtype=jnp.int32)
    placed = orders.astype(jnp.int32)[:, :, None] * BLK + offsets[None, None, :]
    return placed.reshape(SEQS, LEN).astype(jnp.int32)


def block_levels(rng, shape, cuts, low, largest):
    def one(dim, shards_of):
        draws = jax.random.uniform(jax.random.fold_in(jax.random.fold_in(rng, 6), dim), (shards_of,), jnp.float32, low / len(cuts), largest / len(cuts))
        return jnp.repeat(jnp.exp(draws), shape[dim] // shards_of).reshape((-1,) + (1,) * (len(shape) - dim - 1))

    gain = one(*cuts[0])
    for cut in cuts[1:]:
        gain = gain * one(*cut)
    return gain


def noise(stream_key, shape, deviation, reach, cuts=(), kind=jnp.bfloat16):
    array = deviation * jax.random.normal(stream_key, shape, jnp.float32)
    if cuts:
        array = array * block_levels(stream_key, shape, cuts, -0.22, 0.18)
    return jnp.clip(array, -reach, reach).astype(kind)


def setup_inputs(seed: int = 0) -> dict:
    arg_keys = jax.random.split(jax.random.key(seed), 13)
    block_in = noise(arg_keys[0], (SEQS, LEN, D), 1.0, 6.0, ((0, 8), (1, 4)))
    positions = draw_positions(jax.random.fold_in(arg_keys[12], 71), 0)
    norm_attn = jnp.clip(1.0 + 0.1 * jax.random.normal(arg_keys[2], (D,), jnp.float32), 0.5, 1.5).astype(jnp.bfloat16)
    w_query = noise(arg_keys[3], (D, QW), D ** -0.5, 0.125, ((0, 8),))
    key_weight = noise(arg_keys[4], (D, KEY_FEATURES), D ** -0.5, 0.125, ((0, 8),))
    w_value = noise(arg_keys[5], (D, KEY_FEATURES), D ** -0.5, 0.125, ((0, 8),))
    w_out = noise(arg_keys[6], (QW, D), (max(QW // 256, 1)) ** -0.5, 2.0, ((0, 8),))
    norm_ffn = jnp.clip(1.0 + 0.1 * jax.random.normal(arg_keys[7], (D,), jnp.float32), 0.5, 1.5).astype(jnp.bfloat16)
    w_gate = noise(arg_keys[8], (D, FF), D ** -0.5, 0.125, ((0, 8),))
    w_up = noise(arg_keys[9], (D, FF), D ** -0.5, 0.125, ((0, 8),))
    w_down = noise(arg_keys[10], (FF, D), FF ** -0.5, 0.0625, ((0, 8),))
    cotangent = noise(arg_keys[11], (SEQS, LEN, D), 1.0, 6.0, ((0, 8), (1, 4)))
    return dict(block_in=block_in, positions=positions, norm_attn=norm_attn, w_query=w_query, key_weight=key_weight, w_value=w_value, w_out=w_out, norm_ffn=norm_ffn, w_gate=w_gate, w_up=w_up, w_down=w_down, cotangent=cotangent)


@jax.custom_vjp
def low(v):
    return lax.optimization_barrier(v.astype(jnp.bfloat16)).astype(jnp.float32)

@jax.custom_vjp
def low_back(v):
    return v

def low_keep(v):
    return (low(v), None)

def low_pass(kept, grad):
    return (grad,)

def back_keep(v):
    return (v, None)

def back_low(kept, grad):
    return (low(grad),)
low.defvjp(low_keep, low_pass)
low_back.defvjp(back_keep, back_low)
NORM_EPS = 1e-05
ROPE_THETA = 500000.0
NEG_FILL = -1e+30

def matrix_multiply(left_rows, right_rows):
    return jnp.dot(left_rows, right_rows, precision=lax.Precision.HIGHEST, preferred_element_type=jnp.float32)

def angle_tables(position_rows):
    inverse_freq = ROPE_THETA ** (-jnp.arange(HEAD_SIZE // 2, dtype=jnp.float32) * 2.0 / HEAD_SIZE)
    angle_table = position_rows.astype(jnp.float32)[:, None] * inverse_freq[None, :]
    return (jnp.cos(angle_table), jnp.sin(angle_table))

def apply_rotary(field_in, cosine_table, sine_values, heads_count):
    shaped = field_in.reshape(field_in.shape[0], heads_count, HEAD_SIZE)
    leading = shaped[..., :HEAD_SIZE // 2]
    trailing = shaped[..., HEAD_SIZE // 2:]
    cos_part = cosine_table[:, None, :]
    sin_part = sine_values[:, None, :]
    joined = jnp.concatenate([leading * cos_part - trailing * sin_part, trailing * cos_part + leading * sin_part], axis=-1)
    return joined.reshape(field_in.shape)

def rmsnorm(field_in, gain_vec):
    inverse = lax.rsqrt(lax.optimization_barrier(jnp.mean(field_in * field_in, axis=-1, keepdims=True)) + NORM_EPS)
    return field_in * inverse * gain_vec

def attend(operands):
    query_sequence, key_sequence, value_sequence, seq_pos = operands
    sequence_length = query_sequence.shape[0]
    query_head_split = query_sequence.reshape(sequence_length, KEY_VALUE_HEADS, QUERY_HEADS // KEY_VALUE_HEADS, HEAD_SIZE)
    key_head_split = key_sequence.reshape(sequence_length, KEY_VALUE_HEADS, HEAD_SIZE)
    value_head_split = value_sequence.reshape(sequence_length, KEY_VALUE_HEADS, HEAD_SIZE)
    scores = jnp.einsum('tkgd,lkd->kgtl', query_head_split, key_head_split, precision=lax.Precision.HIGHEST)
    scores = low_back(scores * HEAD_SIZE ** (-0.5))
    allowed = seq_pos[None, :] <= seq_pos[:, None]
    scores = jnp.where(allowed[None, None], scores, NEG_FILL)
    row_max = lax.optimization_barrier(jnp.max(scores, axis=-1, keepdims=True))
    weights = jnp.exp(scores - row_max)
    soft_probs = low(weights / lax.optimization_barrier(jnp.sum(weights, axis=-1, keepdims=True)))
    head_out = jnp.einsum('kgtl,lkd->tkgd', soft_probs, value_head_split, precision=lax.Precision.HIGHEST)
    return head_out.reshape(sequence_length, QW)

def forward(positions, in_rows, gain_attn, w_query, key_weight, w_value, w_out, gain_ffn, w_gate, w_up, w_down):
    cosine_table, sine_values = angle_tables(positions.reshape(-1))
    normalized = low(rmsnorm(in_rows, gain_attn))
    query_row_block = low(apply_rotary(low_back(matrix_multiply(normalized, w_query)), cosine_table, sine_values, QUERY_HEADS))
    key_row_block = low(apply_rotary(low_back(matrix_multiply(normalized, key_weight)), cosine_table, sine_values, KEY_VALUE_HEADS))
    value_rows = low(low_back(matrix_multiply(normalized, w_value)))
    attended = lax.map(jax.checkpoint(attend), (query_row_block.reshape(SEQS, LEN, QW), key_row_block.reshape(SEQS, LEN, KEY_FEATURES), value_rows.reshape(SEQS, LEN, KEY_FEATURES), positions))
    attended = low(low_back(attended.reshape(-1, QW)))
    mid_rows = in_rows + low_back(matrix_multiply(attended, w_out))
    normed_ffn = low(rmsnorm(mid_rows, gain_ffn))
    gate_proj = low_back(matrix_multiply(normed_ffn, w_gate))
    up_proj = low_back(matrix_multiply(normed_ffn, w_up))
    hidden = low(jax.nn.silu(gate_proj) * up_proj)
    return mid_rows + low_back(matrix_multiply(hidden, w_down))

def reference(block_in, positions, norm_attn, w_query, key_weight, w_value, w_out, norm_ffn, w_gate, w_up, w_down, cotangent):
    in_rows = block_in.astype(jnp.float32).reshape(-1, D)
    floats = tuple((item.astype(jnp.float32) for item in (norm_attn, w_query, key_weight, w_value, w_out, norm_ffn, w_gate, w_up, w_down)))

    def wrapped(rows_arg, gain_attn, wq_arg, wk_arg, wv_arg, wo_arg, gain_ffn, wg_arg, wu_arg, wd_arg):
        return forward(positions, rows_arg, gain_attn, wq_arg, wk_arg, wv_arg, wo_arg, gain_ffn, wg_arg, wu_arg, wd_arg)
    result, pullback = jax.vjp(wrapped, in_rows, *floats)
    grads = pullback(cotangent.astype(jnp.float32).reshape(-1, D))
    block_out = result.astype(jnp.bfloat16).reshape(block_in.shape)
    input_grad = grads[0].astype(jnp.bfloat16).reshape(block_in.shape)
    return (block_out, input_grad, grads[1], grads[2], grads[3], grads[4], grads[5], grads[6], grads[7], grads[8], grads[9])
```

```python
import jax
import jax.numpy as jnp
from jax import lax
from jax.sharding import PartitionSpec as P

QUERY_HEADS = 32
KEY_VALUE_HEADS = 8
HEAD_SIZE = 64
NORM_EPS = 1e-05
ROPE_THETA = 500000.0
NEG_FILL = -1e30
GROUP = ("dp", "cp")
BF = jnp.bfloat16
F32 = jnp.float32


def matmul(left, right):
    return jnp.dot(left, right, preferred_element_type=F32)


def matmul_nt(left, right):
    return lax.dot_general(left, right, (((1,), (1,)), ((), ())), preferred_element_type=F32)


def matmul_tn(left, right):
    return lax.dot_general(left, right, (((0,), (0,)), ((), ())), preferred_element_type=F32)


def angle_tables(position_rows):
    inverse_freq = ROPE_THETA ** (-jnp.arange(HEAD_SIZE // 2, dtype=F32) * 2.0 / HEAD_SIZE)
    angle_table = position_rows.astype(F32)[:, None] * inverse_freq[None, :]
    return (jnp.cos(angle_table), jnp.sin(angle_table))


def apply_rotary(field_in, cosine_table, sine_values):
    shaped = field_in.reshape(field_in.shape[0], -1, HEAD_SIZE)
    leading = shaped[..., : HEAD_SIZE // 2]
    trailing = shaped[..., HEAD_SIZE // 2 :]
    cos_part = cosine_table[:, None, :]
    sin_part = sine_values[:, None, :]
    joined = jnp.concatenate(
        [leading * cos_part - trailing * sin_part, trailing * cos_part + leading * sin_part],
        axis=-1,
    )
    return joined.reshape(field_in.shape)


def inverse_rms(rows):
    return lax.rsqrt(jnp.mean(rows * rows, axis=-1, keepdims=True) + NORM_EPS)


def rms_back(rows, inverse, gain, grad_rows):
    scaled = grad_rows * gain
    gain_grad = jnp.sum(grad_rows * rows * inverse, axis=0)
    row_inner = jnp.mean(scaled * rows, axis=-1, keepdims=True)
    return (inverse * scaled - rows * inverse * inverse * inverse * row_inner, gain_grad)


def gather(rows):
    return lax.all_gather(rows, GROUP, axis=0, tiled=True)


def scatter(rows):
    return lax.psum_scatter(rows.astype(BF), GROUP, scatter_dimension=0, tiled=True)


def per_device(
    block_in,
    positions,
    norm_attn,
    w_query,
    key_weight,
    w_value,
    w_out,
    norm_ffn,
    w_gate,
    w_up,
    w_down,
    cotangent,
):
    dp = lax.axis_size("dp")
    cp = lax.axis_size("cp")
    n = dp * cp
    tokens, model = block_in.shape[1:]
    length = tokens * cp
    q_heads = QUERY_HEADS // n
    share = max(1, n // KEY_VALUE_HEADS)
    kv_heads = KEY_VALUE_HEADS * share // n
    group = q_heads // kv_heads
    qw, kw = q_heads * HEAD_SIZE, kv_heads * HEAD_SIZE

    x_own = block_in.reshape(tokens, model)
    g_own = cotangent.reshape(tokens, model)
    gain_attn = gather(norm_attn).astype(F32)
    gain_ffn = gather(norm_ffn).astype(F32)
    positions_all = lax.all_gather(positions, "dp", axis=0, tiled=True)
    x_all = gather(x_own)

    def to_columns(weight):
        rows, columns = weight.shape
        return lax.all_to_all(
            weight.reshape(rows, n, columns // n), GROUP, split_axis=1, concat_axis=0, tiled=True
        ).reshape(rows * n, columns // n)

    def to_rows(grad):
        rows, columns = grad.shape
        return lax.all_to_all(
            grad.astype(BF).reshape(rows, 1, columns), GROUP, split_axis=0, concat_axis=1, tiled=True
        ).reshape(rows // n, n * columns)

    rows = w_query.shape[0]

    def spread(weight):
        heads = weight.reshape(rows, KEY_VALUE_HEADS // kv_heads, kw)
        return jnp.repeat(heads, share, axis=1) if share > 1 else heads

    qkv_weight = jnp.concatenate(
        [w_query.reshape(rows, n, qw), spread(key_weight), spread(w_value)], axis=2
    ).reshape(rows, n * (qw + 2 * kw))
    qkv_columns = to_columns(qkv_weight)
    gate_columns = to_columns(w_gate)
    up_columns = to_columns(w_up)

    x_rows = x_all.astype(F32)
    normalized = (x_rows * inverse_rms(x_rows) * gain_attn).astype(BF)
    qkv = matmul(normalized, qkv_columns)
    cosine, sine = angle_tables(positions_all.reshape(-1))
    q = apply_rotary(qkv[:, :qw], cosine, sine).astype(BF)
    k = apply_rotary(qkv[:, qw : qw + kw], cosine, sine).astype(BF)
    v = qkv[:, qw + kw :].astype(BF)
    g_all = gather(g_own)

    def heads_of(x_, heads):
        return x_.reshape(dp, length, kv_heads, heads, HEAD_SIZE)

    allowed = positions_all[:, None, :] <= positions_all[:, :, None]

    def probs_of(q_one, k_one, ok):
        scores = (
            jnp.einsum("tkgd,lkd->kgtl", q_one, k_one, preferred_element_type=F32)
            * HEAD_SIZE ** (-0.5)
        )
        scores = jnp.where(ok, scores, NEG_FILL)
        weights = jnp.exp(scores - jnp.max(scores, axis=-1, keepdims=True))
        return weights / jnp.sum(weights, axis=-1, keepdims=True)

    def attend(operands):
        q_one, k_one, v_one, ok = operands
        probs = probs_of(q_one, k_one, ok).astype(BF)
        return jnp.einsum("kgtl,lkd->tkgd", probs, v_one, preferred_element_type=F32).astype(BF)

    q5, k4, v4 = heads_of(q, group), heads_of(k, 1)[..., 0, :], heads_of(v, 1)[..., 0, :]
    attended = lax.map(attend, (q5, k4, v4, allowed)).reshape(dp * length, qw)
    mid_own = x_own.astype(F32) + scatter(matmul(attended, w_out)).astype(F32)
    inverse_ffn = inverse_rms(mid_own)
    b_own = (mid_own * inverse_ffn * gain_ffn).astype(BF)
    b_all = gather(b_own)
    gate = matmul(b_all, gate_columns)
    up = matmul(b_all, up_columns)
    sigmoid = jax.nn.sigmoid(gate)
    hidden = (gate * sigmoid * up).astype(BF)
    hidden_grad = matmul_nt(g_all, w_down)
    gate_low = (hidden_grad * up * sigmoid * (1.0 + gate * (1.0 - sigmoid))).astype(BF)
    up_low = (hidden_grad * gate * sigmoid).astype(BF)
    ffn_in_grad = scatter(matmul_nt(gate_low, gate_columns) + matmul_nt(up_low, up_columns)).astype(F32)
    down_grad = matmul_tn(hidden, g_all).astype(BF)
    gate_grad = to_rows(matmul_tn(b_all, gate_low))
    up_grad = to_rows(matmul_tn(b_all, up_low))
    block_out = (mid_own + scatter(matmul(hidden, w_down)).astype(F32)).astype(BF)
    mid_part, gain_ffn_grad = rms_back(mid_own, inverse_ffn, gain_ffn, ffn_in_grad)
    mid_grad = g_own.astype(F32) + mid_part
    dr_all = gather(mid_grad.astype(BF))
    out_grad = matmul_tn(attended, dr_all).astype(BF)
    attended_grad = matmul_nt(dr_all, w_out).astype(BF)

    def attend_back(operands):
        q_one, k_one, v_one, ok, do_one = operands
        probs = probs_of(q_one, k_one, ok)
        low = probs.astype(BF)
        prob_grad = jnp.einsum("tkgd,lkd->kgtl", do_one, v_one, preferred_element_type=F32)
        inner = jnp.sum(probs * prob_grad, axis=-1, keepdims=True)
        score = (probs * (prob_grad - inner)).astype(BF)
        scale = HEAD_SIZE ** (-0.5)
        dq = jnp.einsum("kgtl,lkd->tkgd", score, k_one, preferred_element_type=F32) * scale
        dk = jnp.einsum("kgtl,tkgd->lkd", score, q_one, preferred_element_type=F32) * scale
        dv = jnp.einsum("kgtl,tkgd->lkd", low, do_one, preferred_element_type=F32)
        return dq, dk, dv

    dq, dk, dv = lax.map(attend_back, (q5, k4, v4, allowed, heads_of(attended_grad, group)))
    dqkv = jnp.concatenate(
        [
            apply_rotary(dq.reshape(dp * length, qw), cosine, -sine),
            apply_rotary(dk.reshape(dp * length, kw), cosine, -sine),
            dv.reshape(dp * length, kw),
        ],
        axis=1,
    ).astype(BF)
    qkv_grad = to_rows(matmul_tn(normalized, dqkv)).reshape(rows, n, qw + 2 * kw)
    normed_grad = scatter(matmul_nt(dqkv, qkv_columns)).astype(F32)
    in_own = x_own.astype(F32)
    in_part, gain_attn_grad = rms_back(in_own, inverse_rms(in_own), gain_attn, normed_grad)
    input_grad = (mid_grad + in_part).astype(BF)

    def fold(part):
        return part.reshape(rows, -1, share, kw).astype(F32).sum(axis=2).reshape(rows, -1)

    query_grad = qkv_grad[:, :, :qw].reshape(rows, n * qw)
    key_grad = fold(qkv_grad[:, :, qw : qw + kw])
    value_grad = fold(qkv_grad[:, :, qw + kw :])

    def over_rep(part):
        return lax.psum(part.astype(BF), "rep").astype(F32)

    return (
        block_out.reshape(block_in.shape),
        input_grad.reshape(block_in.shape),
        over_rep(scatter(gain_attn_grad)),
        over_rep(query_grad),
        over_rep(key_grad),
        over_rep(value_grad),
        over_rep(out_grad),
        over_rep(scatter(gain_ffn_grad)),
        over_rep(gate_grad),
        over_rep(up_grad),
        over_rep(down_grad),
    )


def solution(mesh):
    rows, both = P(("rep", "dp"), "cp", None), P(GROUP, None)
    return jax.shard_map(
        per_device,
        mesh=mesh,
        in_specs=(
            rows,
            P(("rep", "dp"), None),
            P(GROUP),
            both,
            both,
            both,
            both,
            P(GROUP),
            both,
            both,
            both,
            rows,
        ),
        out_specs=(rows, rows, P(GROUP), both, both, both, both, P(GROUP), both, both, both),
        check_vma=False,
    )
```
